512 devices in a mesh: mp: 16 (over x_lo, y), dp: 32 (over x_hi, z, core).
Axes of the slice: x: 4 (x_hi: 2, x_lo: 2; x = x_hi * 2 + x_lo), y: 8, z: 8, core: 2. Of those that a mesh axis runs over, the one named last changes fastest.
Arguments:
- activations: bfloat16 [16, 2048, 8192], P('mp', 'dp'), may hold values from -54 to 54
- cotangents: bfloat16 [16, 2048, 1792], P('mp', 'dp'), may hold values from -54 to 54
- label_mask: int32 [16, 2048], P('mp', 'dp'), may hold values from 0 to 1, as said below
- checkpoints: bfloat16 [16, 8192, 1792], P('mp', 'dp'), may hold values from -6 to 6
Outputs:
- merged: bfloat16 [8192, 1792], P('dp')
The draws below stay inside these ranges and needn't reach their ends.
Inputs may be any that keep to these rules, and one draw needn't show every extreme that they name: `label_mask`: the last token of every checkpoint is labelled.
All inputs are finite; a program needn't handle non-finite values.
Results may differ from the reference program's by a relative error of at most 0.0025.
Values may be sent and summed in bfloat16 or wider, within the bound.
A program may use at most 64 MiB of HBM per device.

```python
import math
import jax
import jax.numpy as jnp
from jax import lax

D = 8192
FW = 1792
MODELS = 16
TOKENS = 2048


def scaled_field(key, width):
    key_vals, key_rows, key_cols = jax.random.split(key, 3)
    values = jnp.clip(jax.random.normal(key_vals, (MODELS, TOKENS, width), jnp.float32), -6.0, 6.0)
    low_end = math.log(0.3)
    high_end = math.log(3.0)
    row_scale = jnp.exp(jax.random.uniform(key_rows, (MODELS, TOKENS, 1), jnp.float32, low_end, high_end))
    col_scale = jnp.exp(jax.random.uniform(key_cols, (MODELS, 1, width), jnp.float32, low_end, high_end))
    return values * row_scale * col_scale


def draw_activations(key, part):
    return scaled_field(jax.random.fold_in(key, 11), D).astype(jnp.bfloat16)


def draw_cotangents(key, part):
    return scaled_field(jax.random.fold_in(key, 23), FW).astype(jnp.bfloat16)


def draw_label_mask(key, part):
    key_base, key_roll = jax.random.split(jax.random.fold_in(key, 37))
    base_level = jax.random.randint(key_base, (MODELS, 1), 100, 331)
    position = jnp.arange(TOKENS, dtype=jnp.int32)[None, :]
    threshold = base_level * (TOKENS + 2 * position) // TOKENS
    rolled = jax.random.randint(key_roll, (MODELS, TOKENS), 0, 1000)
    labelled = (rolled < threshold).astype(jnp.int32)
    return jnp.where(position == TOKENS - 1, 1, labelled).astype(jnp.int32)


def steps_of(own_key, dims, cuts, least, largest):
    loudness, own = 1.0, jax.random.fold_in(own_key, 6)
    for dim, parts in cuts:
        steps = jnp.exp(jax.random.uniform(jax.random.fold_in(own, dim), (parts,), jnp.float32, least / len(cuts), largest / len(cuts)))
        loudness = loudness * jnp.repeat(steps, dims[dim] // parts).reshape([-1 if axis == dim else 1 for axis in range(len(dims))])
    return loudness


def scatter_about(rng, extent, scale, bound, pieces=(), kind=jnp.bfloat16):
    loudness = steps_of(rng, extent, pieces, -0.22, 0.18) if pieces else 1.0
    entries = jax.random.normal(rng, extent, jnp.float32) * scale * loudness
    return jnp.minimum(jnp.maximum(entries, -bound), bound).astype(kind)


def setup_inputs(seed: int = 0) -> dict:
    keys = jax.random.split(jax.random.key(seed), 5)
    activations = draw_activations(jax.random.fold_in(keys[4], 71), 0)
    cotangents = draw_cotangents(jax.random.fold_in(keys[4], 71), 0)
    label_mask = draw_label_mask(jax.random.fold_in(keys[4], 71), 0)
    checkpoints = scatter_about(keys[3], (MODELS, D, FW), 1.0, 6.0, ((0, 16), (1, 32)))
    return dict(activations=activations, cotangents=cotangents, label_mask=label_mask, checkpoints=checkpoints)


def one_model(totals, inputs):
    tok_acts, tok_cot, tok_mask, slab = inputs
    act_square = jnp.square(tok_acts.astype(jnp.float32)).astype(jnp.bfloat16)
    label_weight = tok_mask.astype(jnp.float32)
    cot_square = (label_weight[:, None] * jnp.square(tok_cot.astype(jnp.float32))).astype(jnp.bfloat16)
    labelled = jnp.sum(label_weight)
    fisher_sum = lax.dot_general(act_square, cot_square, (((0,), (0,)), ((), ())), preferred_element_type=jnp.float32)
    fisher = fisher_sum / labelled
    return (totals[0] + fisher * slab.astype(jnp.float32), totals[1] + fisher), None


def reference(activations, cotangents, label_mask, checkpoints):
    start_sums = (jnp.zeros((D, FW), jnp.float32), jnp.zeros((D, FW), jnp.float32))
    totals, unused = lax.scan(one_model, start_sums, (activations, cotangents, label_mask, checkpoints))
    return (totals[0] / totals[1]).astype(jnp.bfloat16)
```

```python
import functools

import jax
import jax.numpy as jnp
from jax import lax
from jax.experimental import pallas as pl
from jax.experimental.pallas import tpu as pltpu
from jax.sharding import PartitionSpec as P

MESH = pl.DeviceIdType.MESH
BF16 = jnp.bfloat16
F32 = jnp.float32


def near_first(i, n):
    odd = lax.rem(i, 2)
    return odd * lax.div(i + 1, 2) + (1 - odd) * (n - lax.div(i, 2))


def square(x):
    x = x.astype(F32)
    return x * x


def merge_kernel(
    planes, ring, models, chunks,
    act_ref, cot_ref, mask_ref, slab_ref, out_ref,
    act_in, cot_in, act_send, act_all, act_t, cot_all,
    part, part_in, fish_send, fish_all, slab_all, merged,
    count_send, count_all, count_core, count_peer,
    load_sem, act_ssem, act_rsem, slab_ssem, slab_rsem, count_ssem, count_rsem,
    core_ssem, core_rsem, ring_ssem, ring_rsem, flip_rsem, part_ssem, part_rsem,
    fish_ssem, fish_rsem, out_ssem, out_rsem,
):
    group = planes * ring
    tokens = act_in.shape[0]
    feats = act_send.shape[2]
    own_feats = feats // 2
    rows = fish_all.shape[1]
    mp, dp = lax.axis_index("mp"), lax.axis_index("dp")
    core = lax.rem(dp, 2)
    g = lax.div(dp, 2)
    plane, z = lax.div(g, ring), lax.rem(g, ring)

    def in_group(t):
        return (mp, t * 2 + core)

    sibling = (mp, g * 2 + 1 - core)
    flipped = in_group(lax.rem(g + ring, group))
    sides = (
        in_group(plane * ring + lax.rem(z + 1, ring)),
        in_group(plane * ring + lax.rem(z + ring - 1, ring)),
    )

    loads = [
        pltpu.make_async_copy(act_ref, act_in, load_sem.at[0]),
        pltpu.make_async_copy(cot_ref, cot_in, load_sem.at[1]),
    ]
    for load in loads:
        load.start()
    own_slab = pltpu.make_async_copy(
        slab_ref.at[pl.ds(pl.multiple_of(mp * rows, rows), rows), :], slab_all.at[mp], load_sem.at[2]
    )
    own_slab.start()

    barrier = pltpu.get_barrier_semaphore()

    def greet_group(i, c):
        pl.semaphore_signal(barrier, inc=1, device_id=in_group(lax.rem(g + i, group)), device_id_type=MESH)
        return c

    def greet_models(i, c):
        pl.semaphore_signal(barrier, inc=1, device_id=(lax.rem(mp + i, models), dp), device_id_type=MESH)
        return c

    lax.fori_loop(1, group, greet_group, 0)
    lax.fori_loop(1, models, greet_models, 0)
    pl.semaphore_signal(barrier, inc=1, device_id=sibling, device_id_type=MESH)

    loads[1].wait()
    weight = mask_ref[...].astype(F32)
    at_row = lax.broadcasted_iota(jnp.int32, (tokens, tokens), 0)
    at_col = lax.broadcasted_iota(jnp.int32, (tokens, tokens), 1)
    weight_col = jnp.sum(jnp.where(at_row == at_col, weight, 0.0), axis=1, keepdims=True)
    cot_all[g] = (weight_col * square(cot_in[...])).astype(BF16)
    own_count = jnp.sum(weight, axis=1, keepdims=True)
    count_send[...] = jnp.broadcast_to(own_count, count_send.shape)
    count_all[g] = jnp.broadcast_to(own_count, count_send.shape)
    loads[0].wait()

    pl.semaphore_wait(barrier, group + models - 1)

    act_all[g] = square(act_in[:, pl.ds(pl.multiple_of(g * feats, feats), feats)]).astype(BF16)

    def push_act(i, c):
        t = lax.rem(g + near_first(i, group), group)
        act_send[i - 1] = square(act_in[:, pl.ds(pl.multiple_of(t * feats, feats), feats)]).astype(BF16)
        pltpu.make_async_remote_copy(
            act_send.at[i - 1], act_all.at[g], act_ssem, act_rsem, device_id=in_group(t), device_id_type=MESH
        ).start()
        return c

    lax.fori_loop(1, group, push_act, 0)

    def push_count(i, c):
        pltpu.make_async_remote_copy(
            count_send, count_all.at[g], count_ssem, count_rsem,
            device_id=in_group(lax.rem(g + i, group)), device_id_type=MESH,
        ).start()
        return c

    lax.fori_loop(1, group, push_count, 0)

    def push_slab(i, c):
        t = lax.rem(mp + near_first(i, models), models)
        pltpu.make_async_remote_copy(
            slab_ref.at[pl.ds(pl.multiple_of(t * rows, rows), rows), :], slab_all.at[mp],
            slab_ssem, slab_rsem, device_id=(t, dp), device_id_type=MESH,
        ).start()
        return c

    lax.fori_loop(1, models, push_slab, 0)

    starts = [sum(chunks[:k]) for k in range(len(chunks))]
    cols = [pl.ds(s, w) for s, w in zip(starts, chunks)]
    half = ring // 2
    hops = ((half, half - 1), (half - 1, half))

    def flip(k):
        return pltpu.make_async_remote_copy(
            cot_all.at[g, :, cols[k]], cot_all.at[g, :, cols[k]], ring_ssem, flip_rsem.at[k],
            device_id=flipped, device_id_type=MESH,
        )

    def hop(p, side, s, k):
        back = s if side == 0 else ring - s
        owner = lax.rem(plane + p, planes) * ring + lax.rem(z + ring - back, ring) if side == 0 else (
            lax.rem(plane + p, planes) * ring + lax.rem(z + s, ring)
        )
        block = cot_all.at[owner, :, cols[k]]
        return pltpu.make_async_remote_copy(
            block, block, ring_ssem, ring_rsem.at[p, side, s, k], device_id=sides[side], device_id_type=MESH
        )

    def ring_step(s, k):
        if s == 0:
            flip(k).start()
            for side in range(2):
                hop(0, side, 0, k).start()
            return
        for side in range(2):
            if 1 <= s <= hops[0][side]:
                hop(0, side, s - 1, k).wait_recv()
                if s < hops[0][side]:
                    hop(0, side, s, k).start()
        if s == 1:
            flip(k).wait_recv()
        for side in range(2):
            r = s - 1
            if r <= hops[1][side]:
                if r >= 1:
                    hop(1, side, r - 1, k).wait_recv()
                if r < hops[1][side]:
                    hop(1, side, r, k).start()

    last_step = half + 1

    def swap_part(k):
        w = chunks[k]
        return pltpu.make_async_remote_copy(
            part.at[k % 2, pl.ds(pl.multiple_of((1 - core) * own_feats, own_feats), own_feats), pl.ds(0, w)],
            part_in.at[:, cols[k]], part_ssem.at[k], part_rsem.at[k], device_id=sibling, device_id_type=MESH,
        )

    def multiply(k):
        w = chunks[k]
        if k >= 2:
            swap_part(k - 2).wait_send()
        for c in range(0, w, 256):
            block = cot_all[:, :, pl.ds(starts[k] + c, 256)].reshape(group * tokens, 256)
            part[k % 2, :, pl.ds(c, 256)] = jnp.dot(act_t[...], block, preferred_element_type=F32)
        swap_part(k).start()

    def push_fisher(k):
        w = chunks[k]
        swap_part(k).wait_recv()
        labelled = count_core[0:1, 0:1] + count_peer[0:1, 0:1]
        mine = part[k % 2, pl.ds(pl.multiple_of(core * own_feats, own_feats), own_feats), pl.ds(0, w)]
        fisher = ((mine + part_in[:, cols[k]]) / labelled).astype(BF16)
        fish_send[:, :, cols[k]] = fisher.reshape(models, rows, w)
        fish_all[mp, :, cols[k]] = fish_send[mp, :, cols[k]]

        def push(i, c):
            t = lax.rem(mp + near_first(i, models), models)
            pltpu.make_async_remote_copy(
                fish_send.at[t, :, cols[k]], fish_all.at[mp, :, cols[k]], fish_ssem, fish_rsem.at[k],
                device_id=(t, dp), device_id_type=MESH,
            ).start()
            return c

        lax.fori_loop(1, models, push, 0)

    def all_but_one(ref, k):
        return ref.at[pl.ds(0, models - 1), :, cols[k]]

    def wait_bytes(ref, sem):
        pltpu.make_async_copy(ref, ref, sem).wait()

    def merge(k):
        w = chunks[k]
        wait_bytes(all_but_one(fish_all, k), fish_rsem.at[k])
        numerator = jnp.zeros((rows, w), F32)
        denominator = jnp.zeros((rows, w), F32)
        for m in range(models):
            fisher = fish_all[m, :, cols[k]].astype(F32)
            numerator += fisher * slab_all[m, :, cols[k]].astype(F32)
            denominator += fisher
        merged[:, cols[k]] = (numerator / denominator).astype(BF16)

        mine = out_ref.at[pl.ds(pl.multiple_of(mp * rows, rows), rows), cols[k]]
        pltpu.make_async_copy(merged.at[:, cols[k]], mine, load_sem.at[3]).start()

        def push(i, c):
            t = lax.rem(mp + near_first(i, models), models)
            pltpu.make_async_remote_copy(
                merged.at[:, cols[k]], mine, out_ssem, out_rsem, device_id=(t, dp), device_id_type=MESH
            ).start()
            return c

        lax.fori_loop(1, models, push, 0)

    def after_acts():
        wait_bytes(count_all.at[pl.ds(0, group - 1)], count_rsem)
        count_core[...] = jnp.sum(count_all[...], axis=0)
        pltpu.make_async_remote_copy(
            count_core, count_peer, core_ssem, core_rsem, device_id=sibling, device_id_type=MESH
        ).start()
        wait_bytes(act_all.at[pl.ds(0, group - 1)], act_rsem)
        act_t[...] = act_all[...].reshape(group * tokens, feats).T
        wait_bytes(count_peer, core_rsem)
        own_slab.wait()
        wait_bytes(slab_all.at[pl.ds(0, models - 1)], slab_rsem)

    pace = 3
    n = len(chunks)
    last = pace * (n - 1) + last_step + 3
    for tick in range(last + 1):
        for k in range(n):
            s = tick - pace * k
            if 0 <= s <= last_step:
                ring_step(s, k)
        for k in range(n):
            s = tick - pace * k - last_step
            if s == 0:
                if k == 0:
                    after_acts()
                multiply(k)
            elif s == 1:
                push_fisher(k)
            elif s == 3:
                merge(k)

    wait_bytes(act_send, act_ssem)
    wait_bytes(count_all.at[pl.ds(0, group - 1)], count_ssem)
    wait_bytes(count_core, core_ssem)
    wait_bytes(slab_all.at[pl.ds(0, models - 1)], slab_ssem)
    wait_bytes(cot_all.at[pl.ds(0, group - 1)], ring_ssem)
    for k in range(max(0, n - 2), n):
        swap_part(k).wait_send()
    wait_bytes(fish_all.at[pl.ds(0, models - 1)], fish_ssem)
    wait_bytes(merged, load_sem.at[3])
    wait_bytes(fish_all.at[pl.ds(0, models - 1)], out_ssem)
    wait_bytes(out_ref.at[pl.ds(0, (models - 1) * rows), :], out_rsem)


def solution(mesh):
    models = mesh.shape["mp"]
    group = mesh.shape["dp"] // 2
    planes = 2
    ring = group // planes

    def per_device(activations, cotangents, label_mask, checkpoints):
        tokens, width = activations.shape[1:]
        hidden = cotangents.shape[2]
        feats = width // group
        rows = feats // 2 // models
        chunks = [512] * (hidden // 512) + ([hidden % 512] if hidden % 512 else [])
        n = len(chunks)
        dma = pltpu.SemaphoreType.DMA
        hbm = pl.BlockSpec(memory_space=pl.ANY)
        return pl.pallas_call(
            functools.partial(merge_kernel, planes, ring, models, chunks),
            out_shape=jax.ShapeDtypeStruct((feats // 2, hidden), BF16),
            in_specs=[hbm, hbm, pl.BlockSpec(memory_space=pltpu.VMEM), hbm],
            out_specs=hbm,
            scratch_shapes=[
                pltpu.VMEM((tokens, width), BF16),
                pltpu.VMEM((tokens, hidden), BF16),
                pltpu.VMEM((group - 1, tokens, feats), BF16),
                pltpu.VMEM((group, tokens, feats), BF16),
                pltpu.VMEM((feats, group * tokens), BF16),
                pltpu.VMEM((group, tokens, hidden), BF16),
                pltpu.VMEM((2, feats, max(chunks)), F32),
                pltpu.VMEM((feats // 2, hidden), F32),
                pltpu.VMEM((models, rows, hidden), BF16),
                pltpu.VMEM((models, rows, hidden), BF16),
                pltpu.VMEM((models, rows, hidden), BF16),
                pltpu.VMEM((rows, hidden), BF16),
                pltpu.VMEM((8, 128), F32),
                pltpu.VMEM((group, 8, 128), F32),
                pltpu.VMEM((8, 128), F32),
                pltpu.VMEM((8, 128), F32),
                dma((4,)), *[dma(())] * 9,
                dma((2, 2, ring // 2, n)), dma((n,)), dma((n,)), dma((n,)),
                dma(()), dma((n,)), dma(()), dma(()),
            ],
            compiler_params=pltpu.CompilerParams(
                collective_id=0, has_side_effects=True, vmem_limit_bytes=48 << 20
            ),
            name="fisher_merge",
        )(activations[0], cotangents[0], label_mask, checkpoints[0])

    return jax.shard_map(
        per_device,
        mesh=mesh,
        in_specs=(P("mp", "dp", None), P("mp", "dp", None), P("mp", "dp"), P("mp", "dp", None)),
        out_specs=P("dp", None),
        check_vma=False,
    )
```

```python
import functools

import jax
import jax.numpy as jnp
from jax import lax
from jax.experimental import pallas as pl
from jax.experimental.pallas import tpu as pltpu
from jax.sharding import PartitionSpec as P

MESH = pl.DeviceIdType.MESH
BF16 = jnp.bfloat16
F32 = jnp.float32


def near_first(i, n):
    odd = lax.rem(i, 2)
    return odd * lax.div(i + 1, 2) + (1 - odd) * (n - lax.div(i, 2))


def square(x):
    x = x.astype(F32)
    return x * x


def merge_kernel(
    planes, ring, models, chunks,
    act_ref, cot_ref, mask_ref, slab_ref, out_ref,
    act_in, cot_in, act_send, act_all, act_t, cot_all,
    part, part_in, fish_send, fish_all, slab_all, merged,
    count_send, count_all, count_core, count_peer,
    load_sem, act_ssem, act_rsem, slab_ssem, slab_rsem, count_ssem, count_rsem,
    core_ssem, core_rsem, ring_ssem, ring_rsem, flip_rsem, part_ssem, part_rsem,
    fish_ssem, fish_rsem, out_ssem, out_rsem,
):
    group = planes * ring
    tokens = act_in.shape[0]
    feats = act_send.shape[2]
    own_feats = feats // 2
    rows = fish_all.shape[1]
    mp, dp = lax.axis_index("mp"), lax.axis_index("dp")
    core = lax.rem(dp, 2)
    g = lax.div(dp, 2)
    plane, z = lax.div(g, ring), lax.rem(g, ring)

    def in_group(t):
        return (mp, t * 2 + core)

    sibling = (mp, g * 2 + 1 - core)
    flipped = in_group(lax.rem(g + ring, group))
    sides = (
        in_group(plane * ring + lax.rem(z + 1, ring)),
        in_group(plane * ring + lax.rem(z + ring - 1, ring)),
    )

    loads = [
        pltpu.make_async_copy(act_ref, act_in, load_sem.at[0]),
        pltpu.make_async_copy(cot_ref, cot_in, load_sem.at[1]),
    ]
    for load in loads:
        load.start()
    own_slab = pltpu.make_async_copy(
        slab_ref.at[pl.ds(pl.multiple_of(mp * rows, rows), rows), :], slab_all.at[mp], load_sem.at[2]
    )
    own_slab.start()

    barrier = pltpu.get_barrier_semaphore()

    def greet_group(i, c):
        pl.semaphore_signal(barrier, inc=1, device_id=in_group(lax.rem(g + i, group)), device_id_type=MESH)
        return c

    def greet_models(i, c):
        pl.semaphore_signal(barrier, inc=1, device_id=(lax.rem(mp + i, models), dp), device_id_type=MESH)
        return c

    lax.fori_loop(1, group, greet_group, 0)
    lax.fori_loop(1, models, greet_models, 0)
    pl.semaphore_signal(barrier, inc=1, device_id=sibling, device_id_type=MESH)

    loads[1].wait()
    weight = mask_ref[...].astype(F32)
    at_row = lax.broadcasted_iota(jnp.int32, (tokens, tokens), 0)
    at_col = lax.broadcasted_iota(jnp.int32, (tokens, tokens), 1)
    weight_col = jnp.sum(jnp.where(at_row == at_col, weight, 0.0), axis=1, keepdims=True)
    cot_all[g] = (weight_col * square(cot_in[...])).astype(BF16)
    own_count = jnp.sum(weight, axis=1, keepdims=True)
    count_send[...] = jnp.broadcast_to(own_count, count_send.shape)
    count_all[g] = jnp.broadcast_to(own_count, count_send.shape)
    loads[0].wait()

    pl.semaphore_wait(barrier, group + models - 1)

    act_all[g] = square(act_in[:, pl.ds(pl.multiple_of(g * feats, feats), feats)]).astype(BF16)

    def push_act(i, c):
        t = lax.rem(g + near_first(i, group), group)
        act_send[i - 1] = square(act_in[:, pl.ds(pl.multiple_of(t * feats, feats), feats)]).astype(BF16)
        pltpu.make_async_remote_copy(
            act_send.at[i - 1], act_all.at[g], act_ssem, act_rsem, device_id=in_group(t), device_id_type=MESH
        ).start()
        return c

    lax.fori_loop(1, group, push_act, 0)

    def push_count(i, c):
        pltpu.make_async_remote_copy(
            count_send, count_all.at[g], count_ssem, count_rsem,
            device_id=in_group(lax.rem(g + i, group)), device_id_type=MESH,
        ).start()
        return c

    lax.fori_loop(1, group, push_count, 0)

    def push_slab(i, c):
        t = lax.rem(mp + near_first(i, models), models)
        pltpu.make_async_remote_copy(
            slab_ref.at[pl.ds(pl.multiple_of(t * rows, rows), rows), :], slab_all.at[mp],
            slab_ssem, slab_rsem, device_id=(t, dp), device_id_type=MESH,
        ).start()
        return c

    lax.fori_loop(1, models, push_slab, 0)

    starts = [sum(chunks[:k]) for k in range(len(chunks))]
    cols = [pl.ds(s, w) for s, w in zip(starts, chunks)]
    half = ring // 2
    hops = ((half, half - 1), (half - 1, half))

    def flip(k):
        return pltpu.make_async_remote_copy(
            cot_all.at[g, :, cols[k]], cot_all.at[g, :, cols[k]], ring_ssem, flip_rsem.at[k],
            device_id=flipped, device_id_type=MESH,
        )

    def hop(p, side, s, k):
        back = s if side == 0 else ring - s
        owner = lax.rem(plane + p, planes) * ring + lax.rem(z + ring - back, ring) if side == 0 else (
            lax.rem(plane + p, planes) * ring + lax.rem(z + s, ring)
        )
        block = cot_all.at[owner, :, cols[k]]
        return pltpu.make_async_remote_copy(
            block, block, ring_ssem, ring_rsem.at[p, side, s, k], device_id=sides[side], device_id_type=MESH
        )

    def ring_step(s, k):
        if s == 0:
            flip(k).start()
            for side in range(2):
                hop(0, side, 0, k).start()
            return
        for side in range(2):
            if 1 <= s <= hops[0][side]:
                hop(0, side, s - 1, k).wait_recv()
                if s < hops[0][side]:
                    hop(0, side, s, k).start()
        if s == 1:
            flip(k).wait_recv()
        for side in range(2):
            r = s - 1
            if r <= hops[1][side]:
                if r >= 1:
                    hop(1, side, r - 1, k).wait_recv()
                if r < hops[1][side]:
                    hop(1, side, r, k).start()

    last_step = half + 1

    def swap_part(k):
        w = chunks[k]
        return pltpu.make_async_remote_copy(
            part.at[k % 2, pl.ds(pl.multiple_of((1 - core) * own_feats, own_feats), own_feats), pl.ds(0, w)],
            part_in.at[:, cols[k]], part_ssem.at[k], part_rsem.at[k], device_id=sibling, device_id_type=MESH,
        )

    def multiply(k):
        w = chunks[k]
        if k >= 2:
            swap_part(k - 2).wait_send()
        for c in range(0, w, 256):
            block = cot_all[:, :, pl.ds(starts[k] + c, 256)].reshape(group * tokens, 256)
            part[k % 2, :, pl.ds(c, 256)] = jnp.dot(act_t[...], block, preferred_element_type=F32)
        swap_part(k).start()

    def push_fisher(k):
        w = chunks[k]
        swap_part(k).wait_recv()
        labelled = count_core[0:1, 0:1] + count_peer[0:1, 0:1]
        mine = part[k % 2, pl.ds(pl.multiple_of(core * own_feats, own_feats), own_feats), pl.ds(0, w)]
        fisher = ((mine + part_in[:, cols[k]]) / labelled).astype(BF16)
        fish_send[:, :, cols[k]] = fisher.reshape(models, rows, w)
        fish_all[mp, :, cols[k]] = fish_send[mp, :, cols[k]]

        def push(i, c):
            t = lax.rem(mp + near_first(i, models), models)
            pltpu.make_async_remote_copy(
                fish_send.at[t, :, cols[k]], fish_all.at[mp, :, cols[k]], fish_ssem, fish_rsem.at[k],
                device_id=(t, dp), device_id_type=MESH,
            ).start()
            return c

        lax.fori_loop(1, models, push, 0)

    def all_but_one(ref, k):
        return ref.at[pl.ds(0, models - 1), :, cols[k]]

    def wait_bytes(ref, sem):
        pltpu.make_async_copy(ref, ref, sem).wait()

    def merge(k):
        w = chunks[k]
        wait_bytes(all_but_one(fish_all, k), fish_rsem.at[k])
        numerator = jnp.zeros((rows, w), F32)
        denominator = jnp.zeros((rows, w), F32)
        for m in range(models):
            fisher = fish_all[m, :, cols[k]].astype(F32)
            numerator += fisher * slab_all[m, :, cols[k]].astype(F32)
            denominator += fisher
        merged[:, cols[k]] = (numerator / denominator).astype(BF16)

        mine = out_ref.at[pl.ds(pl.multiple_of(mp * rows, rows), rows), cols[k]]
        pltpu.make_async_copy(merged.at[:, cols[k]], mine, load_sem.at[3]).start()

        def push(i, c):
            t = lax.rem(mp + near_first(i, models), models)
            pltpu.make_async_remote_copy(
                merged.at[:, cols[k]], mine, out_ssem, out_rsem, device_id=(t, dp), device_id_type=MESH
            ).start()
            return c

        lax.fori_loop(1, models, push, 0)

    def after_acts():
        wait_bytes(count_all.at[pl.ds(0, group - 1)], count_rsem)
        count_core[...] = jnp.sum(count_all[...], axis=0)
        pltpu.make_async_remote_copy(
            count_core, count_peer, core_ssem, core_rsem, device_id=sibling, device_id_type=MESH
        ).start()
        wait_bytes(act_all.at[pl.ds(0, group - 1)], act_rsem)
        act_t[...] = act_all[...].reshape(group * tokens, feats).T
        wait_bytes(count_peer, core_rsem)
        own_slab.wait()
        wait_bytes(slab_all.at[pl.ds(0, models - 1)], slab_rsem)

    pace = 1
    n = len(chunks)
    last = pace * (n - 1) + last_step + 3
    for tick in range(last + 1):
        for k in range(n):
            s = tick - pace * k
            if 0 <= s <= last_step:
                ring_step(s, k)
        for k in range(n):
            s = tick - pace * k - last_step
            if s == 0:
                if k == 0:
                    after_acts()
                multiply(k)
            elif s == 1:
                push_fisher(k)
            elif s == 3:
                merge(k)

    wait_bytes(act_send, act_ssem)
    wait_bytes(count_all.at[pl.ds(0, group - 1)], count_ssem)
    wait_bytes(count_core, core_ssem)
    wait_bytes(slab_all.at[pl.ds(0, models - 1)], slab_ssem)
    wait_bytes(cot_all.at[pl.ds(0, group - 1)], ring_ssem)
    for k in range(max(0, n - 2), n):
        swap_part(k).wait_send()
    wait_bytes(fish_all.at[pl.ds(0, models - 1)], fish_ssem)
    wait_bytes(merged, load_sem.at[3])
    wait_bytes(fish_all.at[pl.ds(0, models - 1)], out_ssem)
    wait_bytes(out_ref.at[pl.ds(0, (models - 1) * rows), :], out_rsem)


def solution(mesh):
    models = mesh.shape["mp"]
    group = mesh.shape["dp"] // 2
    planes = 2
    ring = group // planes

    def per_device(activations, cotangents, label_mask, checkpoints):
        tokens, width = activations.shape[1:]
        hidden = cotangents.shape[2]
        feats = width // group
        rows = feats // 2 // models
        chunks = [256]*7
        n = len(chunks)
        dma = pltpu.SemaphoreType.DMA
        hbm = pl.BlockSpec(memory_space=pl.ANY)
        return pl.pallas_call(
            functools.partial(merge_kernel, planes, ring, models, chunks),
            out_shape=jax.ShapeDtypeStruct((feats // 2, hidden), BF16),
            in_specs=[hbm, hbm, pl.BlockSpec(memory_space=pltpu.VMEM), hbm],
            out_specs=hbm,
            scratch_shapes=[
                pltpu.VMEM((tokens, width), BF16),
                pltpu.VMEM((tokens, hidden), BF16),
                pltpu.VMEM((group - 1, tokens, feats), BF16),
                pltpu.VMEM((group, tokens, feats), BF16),
                pltpu.VMEM((feats, group * tokens), BF16),
                pltpu.VMEM((group, tokens, hidden), BF16),
                pltpu.VMEM((2, feats, max(chunks)), F32),
                pltpu.VMEM((feats // 2, hidden), F32),
                pltpu.VMEM((models, rows, hidden), BF16),
                pltpu.VMEM((models, rows, hidden), BF16),
                pltpu.VMEM((models, rows, hidden), BF16),
                pltpu.VMEM((rows, hidden), BF16),
                pltpu.VMEM((8, 128), F32),
                pltpu.VMEM((group, 8, 128), F32),
                pltpu.VMEM((8, 128), F32),
                pltpu.VMEM((8, 128), F32),
                dma((4,)), *[dma(())] * 9,
                dma((2, 2, ring // 2, n)), dma((n,)), dma((n,)), dma((n,)),
                dma(()), dma((n,)), dma(()), dma(()),
            ],
            compiler_params=pltpu.CompilerParams(
                collective_id=0, has_side_effects=True, vmem_limit_bytes=62 << 20
            ),
            name="fisher_merge",
        )(activations[0], cotangents[0], label_mask, checkpoints[0])

    return jax.shard_map(
        per_device,
        mesh=mesh,
        in_specs=(P("mp", "dp", None), P("mp", "dp", None), P("mp", "dp"), P("mp", "dp", None)),
        out_specs=P("dp", None),
        check_vma=False,
    )
```

```python
import functools

import jax
import jax.numpy as jnp
from jax import lax
from jax.experimental import pallas as pl
from jax.experimental.pallas import tpu as pltpu
from jax.sharding import PartitionSpec as P

MESH = pl.DeviceIdType.MESH
BF16 = jnp.bfloat16
F32 = jnp.float32


def near_first(i, n):
    odd = lax.rem(i, 2)
    return odd * lax.div(i + 1, 2) + (1 - odd) * (n - lax.div(i, 2))


def square(x):
    x = x.astype(F32)
    return x * x


def merge_kernel(
    planes, ring, models, chunks,
    act_ref, cot_ref, mask_ref, slab_ref, out_ref,
    act_in, cot_in, act_send, act_all, act_t, cot_all,
    part, part_in, fish_send, fish_all, slab_all, merged,
    count_send, count_all, count_core, count_peer,
    load_sem, act_ssem, act_rsem, slab_ssem, slab_rsem, count_ssem, count_rsem,
    core_ssem, core_rsem, ring_ssem, ring_rsem, flip_rsem, part_ssem, part_rsem,
    fish_ssem, fish_rsem, out_ssem, out_rsem,
):
    group = planes * ring
    tokens = act_in.shape[0]
    feats = act_send.shape[2]
    own_feats = feats // 2
    rows = fish_all.shape[1]
    mp, dp = lax.axis_index("mp"), lax.axis_index("dp")
    core = lax.rem(dp, 2)
    g = lax.div(dp, 2)
    plane, z = lax.div(g, ring), lax.rem(g, ring)

    def in_group(t):
        return (mp, t * 2 + core)

    sibling = (mp, g * 2 + 1 - core)
    flipped = in_group(lax.rem(g + ring, group))
    sides = (
        in_group(plane * ring + lax.rem(z + 1, ring)),
        in_group(plane * ring + lax.rem(z + ring - 1, ring)),
    )

    loads = [
        pltpu.make_async_copy(act_ref, act_in, load_sem.at[0]),
        pltpu.make_async_copy(cot_ref, cot_in, load_sem.at[1]),
    ]
    for load in loads:
        load.start()
    own_slab = pltpu.make_async_copy(
        slab_ref.at[pl.ds(pl.multiple_of(mp * rows, rows), rows), :], slab_all.at[mp], load_sem.at[2]
    )
    own_slab.start()

    barrier = pltpu.get_barrier_semaphore()

    def greet_group(i, c):
        pl.semaphore_signal(barrier, inc=1, device_id=in_group(lax.rem(g + i, group)), device_id_type=MESH)
        return c

    def greet_models(i, c):
        pl.semaphore_signal(barrier, inc=1, device_id=(lax.rem(mp + i, models), dp), device_id_type=MESH)
        return c

    lax.fori_loop(1, group, greet_group, 0)
    lax.fori_loop(1, models, greet_models, 0)
    pl.semaphore_signal(barrier, inc=1, device_id=sibling, device_id_type=MESH)

    loads[1].wait()
    weight = mask_ref[...].astype(F32)
    at_row = lax.broadcasted_iota(jnp.int32, (tokens, tokens), 0)
    at_col = lax.broadcasted_iota(jnp.int32, (tokens, tokens), 1)
    weight_col = jnp.sum(jnp.where(at_row == at_col, weight, 0.0), axis=1, keepdims=True)
    cot_all[g] = (weight_col * square(cot_in[...])).astype(BF16)
    own_count = jnp.sum(weight, axis=1, keepdims=True)
    count_send[...] = jnp.broadcast_to(own_count, count_send.shape)
    count_all[g] = jnp.broadcast_to(own_count, count_send.shape)
    loads[0].wait()

    pl.semaphore_wait(barrier, group + models - 1)

    act_all[g] = square(act_in[:, pl.ds(pl.multiple_of(g * feats, feats), feats)]).astype(BF16)

    def push_act(i, c):
        t = lax.rem(g + near_first(i, group), group)
        act_send[i - 1] = square(act_in[:, pl.ds(pl.multiple_of(t * feats, feats), feats)]).astype(BF16)
        pltpu.make_async_remote_copy(
            act_send.at[i - 1], act_all.at[g], act_ssem, act_rsem, device_id=in_group(t), device_id_type=MESH
        ).start()
        return c

    lax.fori_loop(1, group, push_act, 0)

    def push_count(i, c):
        pltpu.make_async_remote_copy(
            count_send, count_all.at[g], count_ssem, count_rsem,
            device_id=in_group(lax.rem(g + i, group)), device_id_type=MESH,
        ).start()
        return c

    lax.fori_loop(1, group, push_count, 0)

    def push_slab(i, c):
        t = lax.rem(mp + near_first(i, models), models)
        pltpu.make_async_remote_copy(
            slab_ref.at[pl.ds(pl.multiple_of(t * rows, rows), rows), :], slab_all.at[mp],
            slab_ssem, slab_rsem, device_id=(t, dp), device_id_type=MESH,
        ).start()
        return c

    lax.fori_loop(1, models, push_slab, 0)

    starts = [sum(chunks[:k]) for k in range(len(chunks))]
    cols = [pl.ds(s, w) for s, w in zip(starts, chunks)]
    half = ring // 2
    hops = ((half, half - 1), (half - 1, half))

    def flip(k):
        return pltpu.make_async_remote_copy(
            cot_all.at[g, :, cols[k]], cot_all.at[g, :, cols[k]], ring_ssem, flip_rsem.at[k],
            device_id=flipped, device_id_type=MESH,
        )

    def hop(p, side, s, k):
        back = s if side == 0 else ring - s
        owner = lax.rem(plane + p, planes) * ring + lax.rem(z + ring - back, ring) if side == 0 else (
            lax.rem(plane + p, planes) * ring + lax.rem(z + s, ring)
        )
        block = cot_all.at[owner, :, cols[k]]
        return pltpu.make_async_remote_copy(
            block, block, ring_ssem, ring_rsem.at[p, side, s, k], device_id=sides[side], device_id_type=MESH
        )

    def ring_step(s, k):
        if s == 0:
            flip(k).start()
            for side in range(2):
                hop(0, side, 0, k).start()
            return
        for side in range(2):
            if 1 <= s <= hops[0][side]:
                hop(0, side, s - 1, k).wait_recv()
                if s < hops[0][side]:
                    hop(0, side, s, k).start()
        if s == 1:
            flip(k).wait_recv()
        for side in range(2):
            r = s - 1
            if r <= hops[1][side]:
                if r >= 1:
                    hop(1, side, r - 1, k).wait_recv()
                if r < hops[1][side]:
                    hop(1, side, r, k).start()

    last_step = half + 1

    def swap_part(k):
        w = chunks[k]
        return pltpu.make_async_remote_copy(
            part.at[k % 2, pl.ds(pl.multiple_of((1 - core) * own_feats, own_feats), own_feats), pl.ds(0, w)],
            part_in.at[:, cols[k]], part_ssem.at[k], part_rsem.at[k], device_id=sibling, device_id_type=MESH,
        )

    def multiply(k):
        w = chunks[k]
        if k >= 2:
            swap_part(k - 2).wait_send()
        for c in range(0, w, 256):
            block = cot_all[:, :, pl.ds(starts[k] + c, 256)].reshape(group * tokens, 256)
            part[k % 2, :, pl.ds(c, 256)] = jnp.dot(act_t[...], block, preferred_element_type=F32)
        swap_part(k).start()

    def push_fisher(k):
        w = chunks[k]
        swap_part(k).wait_recv()
        share = 1.0 / (count_core[0:1, 0:1] + count_peer[0:1, 0:1])
        mine = part[k % 2, pl.ds(pl.multiple_of(core * own_feats, own_feats), own_feats), pl.ds(0, w)]
        fisher = ((mine + part_in[:, cols[k]]) * share).astype(BF16)
        fish_send[:, :, cols[k]] = fisher.reshape(models, rows, w)
        fish_all[mp, :, cols[k]] = fish_send[mp, :, cols[k]]

        def push(i, c):
            t = lax.rem(mp + near_first(i, models), models)
            pltpu.make_async_remote_copy(
                fish_send.at[t, :, cols[k]], fish_all.at[mp, :, cols[k]], fish_ssem, fish_rsem.at[k],
                device_id=(t, dp), device_id_type=MESH,
            ).start()
            return c

        lax.fori_loop(1, models, push, 0)

    def all_but_one(ref, k):
        return ref.at[pl.ds(0, models - 1), :, cols[k]]

    def wait_bytes(ref, sem):
        pltpu.make_async_copy(ref, ref, sem).wait()

    def merge(k):
        w = chunks[k]
        wait_bytes(all_but_one(fish_all, k), fish_rsem.at[k])
        numerator = jnp.zeros((rows, w), F32)
        denominator = jnp.zeros((rows, w), F32)
        for m in range(models):
            fisher = fish_all[m, :, cols[k]].astype(F32)
            numerator += fisher * slab_all[m, :, cols[k]].astype(F32)
            denominator += fisher
        merged[:, cols[k]] = (numerator / denominator).astype(BF16)

        mine = out_ref.at[pl.ds(pl.multiple_of(mp * rows, rows), rows), cols[k]]
        pltpu.make_async_copy(merged.at[:, cols[k]], mine, load_sem.at[3]).start()

        def push(i, c):
            t = lax.rem(mp + near_first(i, models), models)
            pltpu.make_async_remote_copy(
                merged.at[:, cols[k]], mine, out_ssem, out_rsem, device_id=(t, dp), device_id_type=MESH
            ).start()
            return c

        lax.fori_loop(1, models, push, 0)

    def after_acts():
        wait_bytes(count_all.at[pl.ds(0, group - 1)], count_rsem)
        count_core[...] = jnp.sum(count_all[...], axis=0)
        pltpu.make_async_remote_copy(
            count_core, count_peer, core_ssem, core_rsem, device_id=sibling, device_id_type=MESH
        ).start()
        wait_bytes(act_all.at[pl.ds(0, group - 1)], act_rsem)
        act_t[...] = act_all[...].reshape(group * tokens, feats).T
        wait_bytes(count_peer, core_rsem)
        own_slab.wait()
        wait_bytes(slab_all.at[pl.ds(0, models - 1)], slab_rsem)

    pace = 1
    n = len(chunks)
    last = pace * (n - 1) + last_step + 3
    for tick in range(last + 1):
        for k in range(n):
            s = tick - pace * k
            if 0 <= s <= last_step:
                ring_step(s, k)
        for k in range(n):
            if tick - pace * k - last_step == 1:
                push_fisher(k)
        for k in range(n):
            if tick - pace * k - last_step == 0:
                if k == 0:
                    after_acts()
                multiply(k)
        for k in range(n):
            if tick - pace * k - last_step == 2:
                merge(k)

    wait_bytes(act_send, act_ssem)
    wait_bytes(count_all.at[pl.ds(0, group - 1)], count_ssem)
    wait_bytes(count_core, core_ssem)
    wait_bytes(slab_all.at[pl.ds(0, models - 1)], slab_ssem)
    wait_bytes(cot_all.at[pl.ds(0, group - 1)], ring_ssem)
    for k in range(max(0, n - 2), n):
        swap_part(k).wait_send()
    wait_bytes(fish_all.at[pl.ds(0, models - 1)], fish_ssem)
    wait_bytes(merged, load_sem.at[3])
    wait_bytes(fish_all.at[pl.ds(0, models - 1)], out_ssem)
    wait_bytes(out_ref.at[pl.ds(0, (models - 1) * rows), :], out_rsem)


def solution(mesh):
    models = mesh.shape["mp"]
    group = mesh.shape["dp"] // 2
    planes = 2
    ring = group // planes

    def per_device(activations, cotangents, label_mask, checkpoints):
        tokens, width = activations.shape[1:]
        hidden = cotangents.shape[2]
        feats = width // group
        rows = feats // 2 // models
        chunks = [256]*7
        n = len(chunks)
        dma = pltpu.SemaphoreType.DMA
        hbm = pl.BlockSpec(memory_space=pl.ANY)
        return pl.pallas_call(
            functools.partial(merge_kernel, planes, ring, models, chunks),
            out_shape=jax.ShapeDtypeStruct((feats // 2, hidden), BF16),
            in_specs=[hbm, hbm, pl.BlockSpec(memory_space=pltpu.VMEM), hbm],
            out_specs=hbm,
            scratch_shapes=[
                pltpu.VMEM((tokens, width), BF16),
                pltpu.VMEM((tokens, hidden), BF16),
                pltpu.VMEM((group - 1, tokens, feats), BF16),
                pltpu.VMEM((group, tokens, feats), BF16),
                pltpu.VMEM((feats, group * tokens), BF16),
                pltpu.VMEM((group, tokens, hidden), BF16),
                pltpu.VMEM((2, feats, max(chunks)), F32),
                pltpu.VMEM((feats // 2, hidden), F32),
                pltpu.VMEM((models, rows, hidden), BF16),
                pltpu.VMEM((models, rows, hidden), BF16),
                pltpu.VMEM((models, rows, hidden), BF16),
                pltpu.VMEM((rows, hidden), BF16),
                pltpu.VMEM((8, 128), F32),
                pltpu.VMEM((group, 8, 128), F32),
                pltpu.VMEM((8, 128), F32),
                pltpu.VMEM((8, 128), F32),
                dma((4,)), *[dma(())] * 9,
                dma((2, 2, ring // 2, n)), dma((n,)), dma((n,)), dma((n,)),
                dma(()), dma((n,)), dma(()), dma(()),
            ],
            compiler_params=pltpu.CompilerParams(
                collective_id=0, has_side_effects=True, vmem_limit_bytes=62 << 20
            ),
            name="fisher_merge",
        )(activations[0], cotangents[0], label_mask, checkpoints[0])

    return jax.shard_map(
        per_device,
        mesh=mesh,
        in_specs=(P("mp", "dp", None), P("mp", "dp", None), P("mp", "dp"), P("mp", "dp", None)),
        out_specs=P("dp", None),
        check_vma=False,
    )
```

```python
import functools

import jax
import jax.numpy as jnp
from jax import lax
from jax.experimental import pallas as pl
from jax.experimental.pallas import tpu as pltpu
from jax.sharding import PartitionSpec as P

MESH = pl.DeviceIdType.MESH
BF16 = jnp.bfloat16
F32 = jnp.float32


def near_first(i, n):
    odd = lax.rem(i, 2)
    return odd * lax.div(i + 1, 2) + (1 - odd) * (n - lax.div(i, 2))


def square(x):
    x = x.astype(F32)
    return x * x


def merge_kernel(
    planes, ring, models, chunks,
    act_ref, cot_ref, mask_ref, slab_ref, out_ref,
    act_in, cot_in, act_send, act_all, act_t, cot_all,
    part, part_in, fish_send, fish_all, slab_all, merged,
    count_send, count_all, count_core, count_peer,
    load_sem, act_ssem, act_rsem, slab_ssem, slab_rsem, count_ssem, count_rsem,
    core_ssem, core_rsem, ring_ssem, ring_rsem, flip_rsem, part_ssem, part_rsem,
    fish_ssem, fish_rsem, out_ssem, out_rsem,
):
    group = planes * ring
    tokens = act_in.shape[0]
    feats = act_send.shape[2]
    own_feats = feats // 2
    rows = fish_all.shape[1]
    mp, dp = lax.axis_index("mp"), lax.axis_index("dp")
    core = lax.rem(dp, 2)
    g = lax.div(dp, 2)
    plane, z = lax.div(g, ring), lax.rem(g, ring)

    def in_group(t):
        return (mp, t * 2 + core)

    sibling = (mp, g * 2 + 1 - core)
    flipped = in_group(lax.rem(g + ring, group))
    sides = (
        in_group(plane * ring + lax.rem(z + 1, ring)),
        in_group(plane * ring + lax.rem(z + ring - 1, ring)),
    )

    loads = [
        pltpu.make_async_copy(act_ref, act_in, load_sem.at[0]),
        pltpu.make_async_copy(cot_ref, cot_in, load_sem.at[1]),
    ]
    for load in loads:
        load.start()
    own_slab = pltpu.make_async_copy(
        slab_ref.at[pl.ds(pl.multiple_of(mp * rows, rows), rows), :], slab_all.at[mp], load_sem.at[2]
    )
    own_slab.start()

    barrier = pltpu.get_barrier_semaphore()

    def greet_group(i, c):
        pl.semaphore_signal(barrier, inc=1, device_id=in_group(lax.rem(g + i, group)), device_id_type=MESH)
        return c

    def greet_models(i, c):
        pl.semaphore_signal(barrier, inc=1, device_id=(lax.rem(mp + i, models), dp), device_id_type=MESH)
        return c

    lax.fori_loop(1, group, greet_group, 0)
    lax.fori_loop(1, models, greet_models, 0)
    pl.semaphore_signal(barrier, inc=1, device_id=sibling, device_id_type=MESH)

    loads[1].wait()
    weight = mask_ref[...].astype(F32)
    at_row = lax.broadcasted_iota(jnp.int32, (tokens, tokens), 0)
    at_col = lax.broadcasted_iota(jnp.int32, (tokens, tokens), 1)
    weight_col = jnp.sum(jnp.where(at_row == at_col, weight, 0.0), axis=1, keepdims=True)
    cot_all[g] = (weight_col * square(cot_in[...])).astype(BF16)
    own_count = jnp.sum(weight, axis=1, keepdims=True)
    count_send[...] = jnp.broadcast_to(own_count, count_send.shape)
    count_all[g] = jnp.broadcast_to(own_count, count_send.shape)
    loads[0].wait()

    pl.semaphore_wait(barrier, group + models - 1)

    act_all[g] = square(act_in[:, pl.ds(pl.multiple_of(g * feats, feats), feats)]).astype(BF16)

    def push_act(i, c):
        t = lax.rem(g + near_first(i, group), group)
        act_send[i - 1] = square(act_in[:, pl.ds(pl.multiple_of(t * feats, feats), feats)]).astype(BF16)
        pltpu.make_async_remote_copy(
            act_send.at[i - 1], act_all.at[g], act_ssem, act_rsem, device_id=in_group(t), device_id_type=MESH
        ).start()
        return c

    lax.fori_loop(1, group, push_act, 0)

    def push_count(i, c):
        pltpu.make_async_remote_copy(
            count_send, count_all.at[g], count_ssem, count_rsem,
            device_id=in_group(lax.rem(g + i, group)), device_id_type=MESH,
        ).start()
        return c

    lax.fori_loop(1, group, push_count, 0)

    def push_slab(i, c):
        t = lax.rem(mp + near_first(i, models), models)
        pltpu.make_async_remote_copy(
            slab_ref.at[pl.ds(pl.multiple_of(t * rows, rows), rows), :], slab_all.at[mp],
            slab_ssem, slab_rsem, device_id=(t, dp), device_id_type=MESH,
        ).start()
        return c


    starts = [sum(chunks[:k]) for k in range(len(chunks))]
    cols = [pl.ds(s, w) for s, w in zip(starts, chunks)]
    half = ring // 2
    hops = ((half, half - 1), (half - 1, half))

    def flip(k):
        return pltpu.make_async_remote_copy(
            cot_all.at[g, :, cols[k]], cot_all.at[g, :, cols[k]], ring_ssem, flip_rsem.at[k],
            device_id=flipped, device_id_type=MESH,
        )

    def hop(p, side, s, k):
        back = s if side == 0 else ring - s
        owner = lax.rem(plane + p, planes) * ring + lax.rem(z + ring - back, ring) if side == 0 else (
            lax.rem(plane + p, planes) * ring + lax.rem(z + s, ring)
        )
        block = cot_all.at[owner, :, cols[k]]
        return pltpu.make_async_remote_copy(
            block, block, ring_ssem, ring_rsem.at[p, side, s, k], device_id=sides[side], device_id_type=MESH
        )

    def ring_step(s, k):
        if s == 0:
            flip(k).start()
            for side in range(2):
                hop(0, side, 0, k).start()
            return
        for side in range(2):
            if 1 <= s <= hops[0][side]:
                hop(0, side, s - 1, k).wait_recv()
                if s < hops[0][side]:
                    hop(0, side, s, k).start()
        if s == 1:
            flip(k).wait_recv()
        for side in range(2):
            r = s - 1
            if r <= hops[1][side]:
                if r >= 1:
                    hop(1, side, r - 1, k).wait_recv()
                if r < hops[1][side]:
                    hop(1, side, r, k).start()

    last_step = half + 1

    def swap_part(k):
        w = chunks[k]
        return pltpu.make_async_remote_copy(
            part.at[k % 2, pl.ds(pl.multiple_of((1 - core) * own_feats, own_feats), own_feats), pl.ds(0, w)],
            part_in.at[:, cols[k]], part_ssem.at[k], part_rsem.at[k], device_id=sibling, device_id_type=MESH,
        )

    def multiply(k):
        w = chunks[k]
        if k >= 2:
            swap_part(k - 2).wait_send()
        for c in range(0, w, 256):
            block = cot_all[:, :, pl.ds(starts[k] + c, 256)].reshape(group * tokens, 256)
            part[k % 2, :, pl.ds(c, 256)] = jnp.dot(act_t[...], block, preferred_element_type=F32)
        swap_part(k).start()

    def push_fisher(k):
        w = chunks[k]
        swap_part(k).wait_recv()
        share = 1.0 / (count_core[0:1, 0:1] + count_peer[0:1, 0:1])
        mine = part[k % 2, pl.ds(pl.multiple_of(core * own_feats, own_feats), own_feats), pl.ds(0, w)]
        fisher = ((mine + part_in[:, cols[k]]) * share).astype(BF16)
        fish_send[:, :, cols[k]] = fisher.reshape(models, rows, w)
        fish_all[mp, :, cols[k]] = fish_send[mp, :, cols[k]]

        def push(i, c):
            t = lax.rem(mp + near_first(i, models), models)
            pltpu.make_async_remote_copy(
                fish_send.at[t, :, cols[k]], fish_all.at[mp, :, cols[k]], fish_ssem, fish_rsem.at[k],
                device_id=(t, dp), device_id_type=MESH,
            ).start()
            return c

        lax.fori_loop(1, models, push, 0)

    def all_but_one(ref, k):
        return ref.at[pl.ds(0, models - 1), :, cols[k]]

    def wait_bytes(ref, sem):
        pltpu.make_async_copy(ref, ref, sem).wait()

    def merge(k):
        w = chunks[k]
        wait_bytes(all_but_one(fish_all, k), fish_rsem.at[k])
        numerator = jnp.zeros((rows, w), F32)
        denominator = jnp.zeros((rows, w), F32)
        for m in range(models):
            fisher = fish_all[m, :, cols[k]].astype(F32)
            numerator += fisher * slab_all[m, :, cols[k]].astype(F32)
            denominator += fisher
        merged[:, cols[k]] = (numerator / denominator).astype(BF16)

        mine = out_ref.at[pl.ds(pl.multiple_of(mp * rows, rows), rows), cols[k]]
        pltpu.make_async_copy(merged.at[:, cols[k]], mine, load_sem.at[3]).start()

        def push(i, c):
            t = lax.rem(mp + near_first(i, models), models)
            pltpu.make_async_remote_copy(
                merged.at[:, cols[k]], mine, out_ssem, out_rsem, device_id=(t, dp), device_id_type=MESH
            ).start()
            return c

        lax.fori_loop(1, models, push, 0)

    def after_acts():
        wait_bytes(count_all.at[pl.ds(0, group - 1)], count_rsem)
        count_core[...] = jnp.sum(count_all[...], axis=0)
        pltpu.make_async_remote_copy(
            count_core, count_peer, core_ssem, core_rsem, device_id=sibling, device_id_type=MESH
        ).start()
        wait_bytes(act_all.at[pl.ds(0, group - 1)], act_rsem)
        act_t[...] = act_all[...].reshape(group * tokens, feats).T
        wait_bytes(count_peer, core_rsem)
        own_slab.wait()
        wait_bytes(slab_all.at[pl.ds(0, models - 1)], slab_rsem)

    pace = 1
    n = len(chunks)
    last = pace * (n - 1) + last_step + 3
    for tick in range(last + 1):
        if tick == 1:
            lax.fori_loop(1, models, push_slab, 0)
        for k in range(n):
            s = tick - pace * k
            if 0 <= s <= last_step:
                ring_step(s, k)
        for k in range(n):
            if tick - pace * k - last_step == 1:
                push_fisher(k)
        for k in range(n):
            if tick - pace * k - last_step == 0:
                if k == 0:
                    after_acts()
                multiply(k)
        for k in range(n):
            if tick - pace * k - last_step == 2:
                merge(k)

    wait_bytes(act_send, act_ssem)
    wait_bytes(count_all.at[pl.ds(0, group - 1)], count_ssem)
    wait_bytes(count_core, core_ssem)
    wait_bytes(slab_all.at[pl.ds(0, models - 1)], slab_ssem)
    wait_bytes(cot_all.at[pl.ds(0, group - 1)], ring_ssem)
    for k in range(max(0, n - 2), n):
        swap_part(k).wait_send()
    wait_bytes(fish_all.at[pl.ds(0, models - 1)], fish_ssem)
    wait_bytes(merged, load_sem.at[3])
    wait_bytes(fish_all.at[pl.ds(0, models - 1)], out_ssem)
    wait_bytes(out_ref.at[pl.ds(0, (models - 1) * rows), :], out_rsem)


def solution(mesh):
    models = mesh.shape["mp"]
    group = mesh.shape["dp"] // 2
    planes = 2
    ring = group // planes

    def per_device(activations, cotangents, label_mask, checkpoints):
        tokens, width = activations.shape[1:]
        hidden = cotangents.shape[2]
        feats = width // group
        rows = feats // 2 // models
        chunks = [256]*7
        n = len(chunks)
        dma = pltpu.SemaphoreType.DMA
        hbm = pl.BlockSpec(memory_space=pl.ANY)
        return pl.pallas_call(
            functools.partial(merge_kernel, planes, ring, models, chunks),
            out_shape=jax.ShapeDtypeStruct((feats // 2, hidden), BF16),
            in_specs=[hbm, hbm, pl.BlockSpec(memory_space=pltpu.VMEM), hbm],
            out_specs=hbm,
            scratch_shapes=[
                pltpu.VMEM((tokens, width), BF16),
                pltpu.VMEM((tokens, hidden), BF16),
                pltpu.VMEM((group - 1, tokens, feats), BF16),
                pltpu.VMEM((group, tokens, feats), BF16),
                pltpu.VMEM((feats, group * tokens), BF16),
                pltpu.VMEM((group, tokens, hidden), BF16),
                pltpu.VMEM((2, feats, max(chunks)), F32),
                pltpu.VMEM((feats // 2, hidden), F32),
                pltpu.VMEM((models, rows, hidden), BF16),
                pltpu.VMEM((models, rows, hidden), BF16),
                pltpu.VMEM((models, rows, hidden), BF16),
                pltpu.VMEM((rows, hidden), BF16),
                pltpu.VMEM((8, 128), F32),
                pltpu.VMEM((group, 8, 128), F32),
                pltpu.VMEM((8, 128), F32),
                pltpu.VMEM((8, 128), F32),
                dma((4,)), *[dma(())] * 9,
                dma((2, 2, ring // 2, n)), dma((n,)), dma((n,)), dma((n,)),
                dma(()), dma((n,)), dma(()), dma(()),
            ],
            compiler_params=pltpu.CompilerParams(
                collective_id=0, has_side_effects=True, vmem_limit_bytes=62 << 20
            ),
            name="fisher_merge",
        )(activations[0], cotangents[0], label_mask, checkpoints[0])

    return jax.shard_map(
        per_device,
        mesh=mesh,
        in_specs=(P("mp", "dp", None), P("mp", "dp", None), P("mp", "dp"), P("mp", "dp", None)),
        out_specs=P("dp", None),
        check_vma=False,
    )
```
